32 devices in a mesh: ctx: 4 (over y, x), fsdp: 8 (over z, core).
Axes of the slice: x: 2, y: 2, z: 4, core: 2. Of those that a mesh axis runs over, the one named last changes fastest.
Arguments:
- tokens: bfloat16 [16, 1024, 1024], P('fsdp', 'ctx'), may hold values from -6 to 6
- lengths: int32 [16], P('fsdp'), may hold values from 256 to 1024, as said below
- w_query: bfloat16 [1024, 1024], P('fsdp'), may hold values from -0.1875 to 0.1875
- b_query: bfloat16 [1024], P('fsdp'), may hold values from -3 to 3
- w_key: bfloat16 [1024, 1024], P('fsdp'), may hold values from -0.1875 to 0.1875
- w_value: bfloat16 [1024, 1024], P('fsdp'), may hold values from -0.1875 to 0.1875
- b_value: bfloat16 [1024], P('fsdp'), may hold values from -0.119628906 to 0.119628906
- w_output: bfloat16 [1024, 1024], P('fsdp'), may hold values from -1.5 to 1.5
- b_output: bfloat16 [1024], P('fsdp'), may hold values from -2 to 2
- norm1_gain: bfloat16 [1024], P('fsdp'), may hold values from 0.5 to 1.5
- norm1_bias: bfloat16 [1024], P('fsdp'), may hold values from -2 to 2
- w_inner: bfloat16 [1024, 4096], P('fsdp'), may hold values from -0.1875 to 0.1875
- b_inner: bfloat16 [4096], P('fsdp'), may hold values from -3 to 3
- w_outer: bfloat16 [4096, 1024], P('fsdp'), may hold values from -0.09375 to 0.09375
- b_outer: bfloat16 [1024], P('fsdp'), may hold values from -2 to 2
- norm2_gain: bfloat16 [1024], P('fsdp'), may hold values from 0.5 to 1.5
- norm2_bias: bfloat16 [1024], P('fsdp'), may hold values from -2 to 2
- cotangent: bfloat16 [16, 1024, 1024], P('fsdp', 'ctx'), may hold values from -6 to 6
Outputs:
- output: bfloat16 [16, 1024, 1024], P('fsdp', 'ctx')
- grad_tokens: float32 [16, 1024, 1024], P('fsdp', 'ctx')
- grad_w_query: float32 [1024, 1024], P('fsdp')
- grad_b_query: float32 [1024], P('fsdp')
- grad_w_key: float32 [1024, 1024], P('fsdp')
- grad_w_value: float32 [1024, 1024], P('fsdp')
- grad_b_value: float32 [1024], P('fsdp')
- grad_w_output: float32 [1024, 1024], P('fsdp')
- grad_b_output: float32 [1024], P('fsdp')
- grad_norm1_gain: float32 [1024], P('fsdp')
- grad_norm1_bias: float32 [1024], P('fsdp')
- grad_w_inner: float32 [1024, 4096], P('fsdp')
- grad_b_inner: float32 [4096], P('fsdp')
- grad_w_outer: float32 [4096, 1024], P('fsdp')
- grad_b_outer: float32 [1024], P('fsdp')
- grad_norm2_gain: float32 [1024], P('fsdp')
- grad_norm2_bias: float32 [1024], P('fsdp')
The draws below stay inside these ranges and needn't reach their ends.
Inputs may be any that keep to these rules, and one draw needn't show every extreme that they name: lengths[s] is the count of real tokens of sequence s; some sequence has exactly 1024 and some exactly 256.
All inputs are finite; a program needn't handle non-finite values.
Results may differ from the reference program's by a relative error of at most 0.02.
Values may be sent and summed in bfloat16 or wider, within the bound.
No kernel may reach another device: no remote copies, remote signals or barrier semaphores. Data moves between devices by JAX's collectives and lax.ppermute only.
A program may use at most 320 MiB of HBM per device.

```python
import jax
import jax.numpy as jnp
from jax import lax

D = 1024
HEADS = 16
HEAD_DIM = 64
FF = 4096
LEN = 1024
SEQUENCES = 16


def draw_lengths(key, part):
    drawn = jax.random.randint(jax.random.fold_in(key, 11), (SEQUENCES,), LEN // 4, LEN + 1)
    longest = jax.random.randint(jax.random.fold_in(key, 12), (), 0, SEQUENCES)
    offset = jax.random.randint(jax.random.fold_in(key, 13), (), 0, SEQUENCES - 1)
    shortest = (longest + 1 + offset) % SEQUENCES
    indices = jnp.arange(SEQUENCES)
    drawn = jnp.where(indices == longest, LEN, drawn)
    drawn = jnp.where(indices == shortest, LEN // 4, drawn)
    return drawn.astype(jnp.int32)


def levels(stream_key, extent, split, least, top_value):
    def one(dim, parts):
        draws = jax.random.uniform(jax.random.fold_in(jax.random.fold_in(stream_key, 6), dim), (parts,), jnp.float32, least / len(split), top_value / len(split))
        return jnp.repeat(jnp.exp(draws), extent[dim] // parts).reshape((-1,) + (1,) * (len(extent) - dim - 1))

    level = one(*split[0])
    for cut in split[1:]:
        level = level * one(*cut)
    return level


def normal_values(rng, shape, deviation, reach, split=(), kind=jnp.bfloat16):
    loudness = levels(rng, shape, split, -0.22, 0.18) if split else 1.0
    values = jax.random.normal(rng, shape, jnp.float32) * deviation * loudness
    return jnp.minimum(jnp.maximum(values, -reach), reach).astype(kind)


def setup_inputs(seed: int = 0) -> dict:
    key_list = jax.random.split(jax.random.key(seed), 19)
    tokens = normal_values(key_list[0], (SEQUENCES, LEN, D), 1.0, 6.0, ((0, 8), (1, 4)))
    lengths = draw_lengths(jax.random.fold_in(key_list[18], 71), 0)
    w_query = normal_values(key_list[2], (D, D), D ** -0.5, 0.1875, ((0, 8),))
    b_query = normal_values(key_list[3], (D,), 0.5, 3.0, ((0, 8),))
    w_key = normal_values(key_list[4], (D, D), D ** -0.5, 0.1875, ((0, 8),))
    w_value = normal_values(key_list[5], (D, D), D ** -0.5, 0.1875, ((0, 8),))
    b_value = normal_values(key_list[6], (D,), 0.02, 0.119628906, ((0, 8),))
    w_output = normal_values(key_list[7], (D, D), (max(1, 16 * D // LEN)) ** -0.5, 1.5, ((0, 8),))
    b_output = normal_values(key_list[8], (D,), 0.3, 2.0, ((0, 8),))
    norm1_gain = jnp.clip(1.0 + 0.1 * jax.random.normal(key_list[9], (D,), jnp.float32), 0.5, 1.5).astype(jnp.bfloat16)
    norm1_bias = normal_values(key_list[10], (D,), 0.3, 2.0, ((0, 8),))
    w_inner = normal_values(key_list[11], (D, FF), D ** -0.5, 0.1875, ((0, 8),))
    b_inner = normal_values(key_list[12], (FF,), 0.5, 3.0, ((0, 8),))
    w_outer = normal_values(key_list[13], (FF, D), FF ** -0.5, 0.09375, ((0, 8),))
    b_outer = normal_values(key_list[14], (D,), 0.3, 2.0, ((0, 8),))
    norm2_gain = jnp.clip(1.0 + 0.1 * jax.random.normal(key_list[15], (D,), jnp.float32), 0.5, 1.5).astype(jnp.bfloat16)
    norm2_bias = normal_values(key_list[16], (D,), 0.3, 2.0, ((0, 8),))
    cotangent = normal_values(key_list[17], (SEQUENCES, LEN, D), 1.0, 6.0, ((0, 8), (1, 4)))
    return {"tokens": tokens, "lengths": lengths, "w_query": w_query, "b_query": b_query, "w_key": w_key, "w_value": w_value, "b_value": b_value, "w_output": w_output, "b_output": b_output, "norm1_gain": norm1_gain, "norm1_bias": norm1_bias, "w_inner": w_inner, "b_inner": b_inner, "w_outer": w_outer, "b_outer": b_outer, "norm2_gain": norm2_gain, "norm2_bias": norm2_bias, "cotangent": cotangent}


EPSILON = 1e-12
ROOT_HALF = 0.7071067811865476
NEGATIVE = -1e+30
HIGHEST_PRECISION = lax.Precision.HIGHEST

@jax.custom_vjp
def low(v):
    return lax.optimization_barrier(v.astype(jnp.bfloat16)).astype(jnp.float32)

@jax.custom_vjp
def low_back(v):
    return v

def low_keep(v):
    return (low(v), None)

def low_pass(kept, grad):
    return (grad,)

def back_keep(v):
    return (v, None)

def back_low(kept, grad):
    return (low(grad),)
low.defvjp(low_keep, low_pass)
low_back.defvjp(back_keep, back_low)

def product(left, right):
    return jnp.dot(left, right, precision=HIGHEST_PRECISION)

def layer_norm(hidden, gain_vec, offset):
    center = hidden - lax.optimization_barrier(jnp.mean(hidden, axis=-1, keepdims=True))
    variance = lax.optimization_barrier(jnp.mean(center * center, axis=-1, keepdims=True))
    return center * lax.rsqrt(variance + EPSILON) * gain_vec + offset

def forward(inputs, key_valid, w_query, b_query, w_key, w_value, b_value, w_output, b_output, norm1_gain, norm1_bias, w_inner, b_inner, w_outer, b_outer, norm2_gain, norm2_bias):
    seq_len = inputs.shape[0]
    score_scale = HEAD_DIM ** (-0.5)
    rounded = low(inputs)
    query_low = low(low_back(product(rounded, w_query) + b_query)).reshape(seq_len, HEADS, HEAD_DIM)
    key_proj = low(low_back(product(rounded, w_key))).reshape(seq_len, HEADS, HEAD_DIM)
    value_proj = low(low_back(product(rounded, w_value) + b_value)).reshape(seq_len, HEADS, HEAD_DIM)
    scores = low_back(jnp.einsum('qhd,khd->hqk', query_low, key_proj, precision=HIGHEST_PRECISION) * score_scale)
    scores = jnp.where(key_valid[None, None, :], scores, NEGATIVE)
    weights = low(jax.nn.softmax(scores, axis=-1))
    attended = jnp.einsum('hqk,khd->qhd', weights, value_proj, precision=HIGHEST_PRECISION)
    attended = low(low_back(attended.reshape(seq_len, HEADS * HEAD_DIM)))
    branch = low_back(product(attended, w_output) + b_output)
    layer_mid = layer_norm(inputs + branch, norm1_gain, norm1_bias)
    pre_act = low_back(product(low(layer_mid), w_inner) + b_inner)
    activated = low(0.5 * pre_act * (1.0 + lax.erf(pre_act * ROOT_HALF)))
    feed_out = low_back(product(activated, w_outer) + b_outer)
    return layer_norm(layer_mid + feed_out, norm2_gain, norm2_bias)

def reference(tokens, lengths, w_query, b_query, w_key, w_value, b_value, w_output, b_output, norm1_gain, norm1_bias, w_inner, b_inner, w_outer, b_outer, norm2_gain, norm2_bias, cotangent):
    params = tuple((tensor.astype(jnp.float32) for tensor in (w_query, b_query, w_key, w_value, b_value, w_output, b_output, norm1_gain, norm1_bias, w_inner, b_inner, w_outer, b_outer, norm2_gain, norm2_bias)))
    positions = jnp.arange(LEN, dtype=jnp.int32)

    def one_sequence(running, packed):
        inputs, length, grad_out = packed
        key_valid = positions < length

        def apply_layer(layer_in, *weight_list):
            return forward(layer_in, key_valid, *weight_list)
        result, pull_back = jax.vjp(apply_layer, inputs.astype(jnp.float32), *params)
        grad_all = pull_back(grad_out.astype(jnp.float32))
        updated = tuple((total_grad + grad_part for total_grad, grad_part in zip(running, grad_all[1:])))
        return (updated, (result.astype(jnp.bfloat16), grad_all[0]))
    zeros_init = tuple((jnp.zeros(tensor.shape, jnp.float32) for tensor in params))
    grad_sums, (outputs, grad_inputs) = lax.scan(one_sequence, zeros_init, (tokens, lengths, cotangent))
    return (outputs, grad_inputs, grad_sums[0], grad_sums[1], grad_sums[2], grad_sums[3], grad_sums[4], grad_sums[5], grad_sums[6], grad_sums[7], grad_sums[8], grad_sums[9], grad_sums[10], grad_sums[11], grad_sums[12], grad_sums[13], grad_sums[14])
```

```python
import functools

import jax
import jax.numpy as jnp
from jax import lax
from jax.experimental import pallas as pl
from jax.experimental.pallas import tpu as pltpu
from jax.sharding import PartitionSpec as P

HEAD_DIM = 64
LANES = 128
EPSILON = 1e-12
ROOT_HALF = 0.7071067811865476
INV_ROOT_TWO_PI = 0.3989422804014327
NEGATIVE = -1e30
BF16 = jnp.bfloat16
F32 = jnp.float32


def normalize(hidden):
    center = hidden - jnp.mean(hidden, axis=-1, keepdims=True)
    variance = jnp.mean(center * center, axis=-1, keepdims=True)
    inverse = lax.rsqrt(variance + EPSILON)
    return (center * inverse, inverse)


def norm_back(grad_norm, normed, inverse):
    mean_grad = jnp.mean(grad_norm, axis=-1, keepdims=True)
    mean_cross = jnp.mean(grad_norm * normed, axis=-1, keepdims=True)
    return inverse * (grad_norm - mean_grad - normed * mean_cross)


def dot_nn(left, right):
    return lax.dot_general(left, right, (((1,), (0,)), ((), ())), preferred_element_type=F32)


def dot_nt(left, right):
    return lax.dot_general(left, right, (((1,), (1,)), ((), ())), preferred_element_type=F32)


def dot_tn(left, right):
    return lax.dot_general(left, right, (((0,), (0,)), ((), ())), preferred_element_type=F32)


def key_bias(scalars, shape, axis, local_len):
    index = lax.broadcasted_iota(jnp.int32, shape, axis)
    owner = jnp.bitwise_xor(scalars[0], index // local_len)
    position = owner * local_len + index % local_len
    return jnp.where(position < scalars[1], 0.0, NEGATIVE).astype(F32)


def head_lanes(values, head):
    lane = lax.broadcasted_iota(jnp.int32, values.shape, 1)
    return jnp.where(lane // HEAD_DIM == head, values, jnp.zeros_like(values))


def attend_kernel(scalars, qkv_ref, out_ref, *, local_len, block):
    total = qkv_ref.shape[0]
    bias = key_bias(scalars, (1, total), 1, local_len)
    keys = qkv_ref[:, LANES : 2 * LANES]
    values = qkv_ref[:, 2 * LANES :]
    masked_values = [head_lanes(values, h) for h in range(2)]

    def step(i, carry):
        rows = pl.ds(pl.multiple_of(i * block, block), block)
        query = qkv_ref[rows, :LANES] * jnp.asarray(HEAD_DIM ** (-0.5), BF16)
        out = None
        for h in range(2):
            scores = dot_nt(head_lanes(query, h), keys) + bias
            top = jnp.max(scores, axis=-1, keepdims=True)
            raw = jnp.exp(scores - top)
            scale = 1.0 / jnp.sum(raw, axis=-1, keepdims=True)
            part = dot_nn((raw * scale).astype(BF16), masked_values[h])
            out = part if out is None else out + part
        out_ref[rows, :] = out.astype(BF16)
        return carry

    lax.fori_loop(0, total // block, step, 0)


def attend_back_kernel(scalars, qkv_ref, grad_ref, out_ref, key_acc, value_acc, *, local_len, block):
    total = qkv_ref.shape[0]
    score_scale = HEAD_DIM ** (-0.5)
    bias = key_bias(scalars, (total, 1), 0, local_len)
    keys = qkv_ref[:, LANES : 2 * LANES]
    values = qkv_ref[:, 2 * LANES :]
    masked_keys = [head_lanes(keys, h) for h in range(2)]
    key_acc[...] = jnp.zeros_like(key_acc)
    value_acc[...] = jnp.zeros_like(value_acc)

    def step(i, carry):
        rows = pl.ds(pl.multiple_of(i * block, block), block)
        query = qkv_ref[rows, :LANES] * jnp.asarray(score_scale, BF16)
        grad = grad_ref[rows, :]
        grad_query = None
        grad_key = None
        grad_value = None
        for h in range(2):
            query_h = head_lanes(query, h)
            grad_h = head_lanes(grad, h)
            scores = dot_nt(keys, query_h) + bias
            top = jnp.max(scores, axis=0, keepdims=True)
            raw = jnp.exp(scores - top)
            weights = raw * (1.0 / jnp.sum(raw, axis=0, keepdims=True))
            grad_probs = dot_nt(values, grad_h)
            inner = jnp.sum(weights * grad_probs, axis=0, keepdims=True)
            grad_scores = (weights * (grad_probs - inner)).astype(BF16)
            part_v = dot_nn(weights.astype(BF16), grad_h)
            part_k = dot_nn(grad_scores, query_h)
            part_q = dot_tn(grad_scores, masked_keys[h])
            grad_value = part_v if h == 0 else grad_value + part_v
            grad_key = part_k if h == 0 else grad_key + part_k
            grad_query = part_q if h == 0 else grad_query + part_q
        out_ref[rows, :LANES] = (grad_query * score_scale).astype(BF16)
        key_acc[...] += grad_key
        value_acc[...] += grad_value
        return carry

    lax.fori_loop(0, total // block, step, 0)
    out_ref[:, LANES : 2 * LANES] = key_acc[...].astype(BF16)
    out_ref[:, 2 * LANES :] = value_acc[...].astype(BF16)


def attend(scalars, qkv, local_len):
    total, width = qkv.shape
    pairs = width // (3 * LANES)
    return pl.pallas_call(
        functools.partial(attend_kernel, local_len=local_len, block=256),
        grid_spec=pltpu.PrefetchScalarGridSpec(
            num_scalar_prefetch=1,
            grid=(pairs,),
            in_specs=[pl.BlockSpec((total, 3 * LANES), lambda j, s: (0, j))],
            out_specs=pl.BlockSpec((total, LANES), lambda j, s: (0, j)),
        ),
        out_shape=jax.ShapeDtypeStruct((total, pairs * LANES), BF16),
        name="attend",
    )(scalars, qkv)


def attend_back(scalars, qkv, grad, local_len):
    total, width = qkv.shape
    pairs = width // (3 * LANES)
    return pl.pallas_call(
        functools.partial(attend_back_kernel, local_len=local_len, block=256),
        grid_spec=pltpu.PrefetchScalarGridSpec(
            num_scalar_prefetch=1,
            grid=(pairs,),
            in_specs=[
                pl.BlockSpec((total, 3 * LANES), lambda j, s: (0, j)),
                pl.BlockSpec((total, LANES), lambda j, s: (0, j)),
            ],
            out_specs=pl.BlockSpec((total, 3 * LANES), lambda j, s: (0, j)),
            scratch_shapes=[pltpu.VMEM((total, LANES), F32), pltpu.VMEM((total, LANES), F32)],
        ),
        out_shape=jax.ShapeDtypeStruct((total, width), BF16),
        name="attend_back",
    )(scalars, qkv, grad)


def body(
    ctx_size,
    fsdp_size,
    tokens,
    lengths,
    w_query,
    b_query,
    w_key,
    w_value,
    b_value,
    w_output,
    b_output,
    norm1_gain,
    norm1_bias,
    w_inner,
    b_inner,
    w_outer,
    b_outer,
    norm2_gain,
    norm2_bias,
    cotangent,
):
    place = lax.axis_index("ctx")
    half = place % 2
    seqs, local, width = tokens.shape
    shard = width // fsdp_size
    columns = width // ctx_size
    pairs = columns // LANES
    hidden = w_inner.shape[1]
    hidden_shard = hidden // fsdp_size
    hidden_part = hidden_shard // 2
    masks = range(ctx_size)

    def swap(value, mask):
        return lax.ppermute(value, "ctx", [(i, i ^ mask) for i in range(ctx_size)])

    def head_columns(weight):
        mine = lax.dynamic_slice_in_dim(weight, place * columns, columns, 1)
        return mine.reshape(shard, pairs, LANES)

    qkv_shard = jnp.stack(
        [head_columns(w_query), head_columns(w_key), head_columns(w_value)], axis=2
    ).reshape(shard, 3 * columns)
    small = jnp.concatenate(
        [b_query, b_value, b_output, norm1_gain, norm1_bias, b_outer, norm2_gain, norm2_bias, b_inner]
    )
    small_len = small.shape[0]
    small_rows = -(-small_len // (3 * columns))
    small_rows = -(-small_rows // 16) * 16
    small = jnp.pad(small, (0, small_rows * 3 * columns - small_len)).reshape(small_rows, 3 * columns)
    first = lax.all_gather(jnp.concatenate([qkv_shard, small], axis=0), "fsdp", axis=0, tiled=True)
    first = first.reshape(fsdp_size, shard + small_rows, 3 * columns)
    qkv_full = first[:, :shard].reshape(width, 3 * columns)
    small_full = first[:, shard:].reshape(fsdp_size, -1).astype(F32)
    vectors = [small_full[:, i * shard : (i + 1) * shard].reshape(width) for i in range(8)]
    query_bias, value_bias, output_bias, gain_one, bias_one, outer_bias, gain_two, bias_two = vectors
    inner_bias = lax.dynamic_index_in_dim(
        small_full[:, 8 * shard : 8 * shard + hidden_shard].reshape(fsdp_size, 2, hidden_part),
        half,
        1,
        keepdims=False,
    ).reshape(fsdp_size * hidden_part)

    def own_bias(vector):
        return lax.dynamic_slice_in_dim(vector, place * columns, columns, 0).reshape(pairs, LANES)

    q_bias, v_bias = (own_bias(query_bias), own_bias(value_bias))
    qkv_bias = jnp.stack([q_bias, jnp.zeros_like(q_bias), v_bias], axis=1).reshape(3 * columns)

    output_full = lax.all_gather(w_output, "fsdp", axis=0, tiled=True)
    inner_half = lax.dynamic_index_in_dim(
        w_inner.reshape(shard, fsdp_size, 2, hidden_part), half, 2, keepdims=False
    ).reshape(shard, fsdp_size * hidden_part)
    inner_full = lax.all_gather(inner_half, "fsdp", axis=0, tiled=True)
    outer_half = lax.dynamic_slice_in_dim(w_outer, half * hidden_part, hidden_part, 0)
    outer_full = lax.all_gather(outer_half, "fsdp", axis=0, tiled=True)

    inputs_all, qkv_all, scalars, attn_all = ([], [], [], [])
    for s in range(seqs):
        pieces = [tokens[s] if m == 0 else swap(tokens[s], m) for m in masks]
        inputs_all.append(jnp.concatenate(pieces, axis=0))
        qkv = (dot_nn(inputs_all[s], qkv_full) + qkv_bias).astype(BF16)
        qkv_all.append(qkv)
        scalars.append(jnp.stack([place.astype(jnp.int32), lengths[s]]))
        heads_out = attend(scalars[s], qkv, local)
        attn = jnp.zeros((local, width), BF16)
        for m in masks:
            piece = heads_out[m * local : (m + 1) * local]
            piece = piece if m == 0 else swap(piece, m)
            attn = lax.dynamic_update_slice_in_dim(attn, piece, (place ^ m) * columns, 1)
        attn_all.append(attn)

    saved = []
    for s in range(seqs):
        branch = dot_nn(attn_all[s], output_full) + output_bias
        normed_one, inverse_one = normalize(tokens[s].astype(F32) + branch)
        layer_mid = normed_one * gain_one + bias_one
        mid_low = layer_mid.astype(BF16)
        mids = [mid_low, swap(mid_low, 1)]
        acts, slopes = ([], [])
        for rows in mids:
            pre_act = dot_nn(rows, inner_full) + inner_bias
            erf_part = lax.erf(pre_act * ROOT_HALF)
            acts.append((0.5 * pre_act * (1.0 + erf_part)).astype(BF16))
            slopes.append(
                (
                    0.5 * (1.0 + erf_part)
                    + pre_act * jnp.exp(-0.5 * pre_act * pre_act) * INV_ROOT_TWO_PI
                ).astype(BF16)
            )
        other = swap(dot_nn(acts[1], outer_full).astype(BF16), 1)
        feed_out = dot_nn(acts[0], outer_full) + other.astype(F32) + outer_bias
        normed_two, inverse_two = normalize(layer_mid + feed_out)
        result = (normed_two * gain_two + bias_two).astype(BF16)
        saved.append((normed_one, inverse_one, mids, acts, slopes, normed_two, inverse_two, result))

    sums = {name: [] for name in ("g2", "b2", "bo", "bi", "g1", "b1", "bout")}
    feeds, pres, branches, resid_ones = ([], [], [], [])
    for s in range(seqs):
        normed_one, inverse_one, mids, acts, slopes, normed_two, inverse_two, _ = saved[s]
        grad_out = cotangent[s].astype(F32)
        sums["g2"].append(jnp.sum(grad_out * normed_two, axis=0))
        sums["b2"].append(jnp.sum(grad_out, axis=0))
        grad_resid_two = norm_back(grad_out * gain_two, normed_two, inverse_two)
        grad_feed = grad_resid_two.astype(BF16)
        sums["bo"].append(jnp.sum(grad_feed, axis=0, dtype=F32))
        grads = [grad_feed, swap(grad_feed, 1)]
        feeds += grads
        pre = [
            (dot_nt(grads[i], outer_full) * slopes[i].astype(F32)).astype(BF16) for i in range(2)
        ]
        pres += pre
        for value in pre:
            sums["bi"].append(jnp.sum(value, axis=0, dtype=F32))
        other = swap(dot_nt(pre[1], inner_full).astype(BF16), 1)
        grad_mid = grad_resid_two + dot_nt(pre[0], inner_full) + other.astype(F32)
        sums["g1"].append(jnp.sum(grad_mid * normed_one, axis=0))
        sums["b1"].append(jnp.sum(grad_mid, axis=0))
        grad_resid_one = norm_back(grad_mid * gain_one, normed_one, inverse_one)
        grad_branch = grad_resid_one.astype(BF16)
        sums["bout"].append(jnp.sum(grad_branch, axis=0, dtype=F32))
        resid_ones.append(grad_resid_one)
        branches.append(grad_branch)

    def rows_of(parts):
        return jnp.concatenate(parts, axis=0)

    def scatter(grad):
        return lax.psum_scatter(grad.astype(BF16), "fsdp", scatter_dimension=0, tiled=True)

    act_rows = rows_of([a for s in range(seqs) for a in saved[s][3]])
    mid_rows = rows_of([a for s in range(seqs) for a in saved[s][2]])
    outer_shard = scatter(dot_tn(act_rows, rows_of(feeds)))
    inner_shard = scatter(dot_tn(mid_rows, rows_of(pres)))
    output_shard = scatter(dot_tn(rows_of(attn_all), rows_of(branches)))

    grad_qkv_all, grad_tokens = ([], [])
    for s in range(seqs):
        grad_attn = dot_nt(branches[s], output_full).astype(BF16)
        pieces = []
        for m in masks:
            piece = lax.dynamic_slice_in_dim(grad_attn, (place ^ m) * columns, columns, 1)
            pieces.append(piece if m == 0 else swap(piece, m))
        grad_qkv = attend_back(scalars[s], qkv_all[s], rows_of(pieces), local)
        grad_qkv_all.append(grad_qkv)
        total = resid_ones[s]
        for m in reversed(masks):
            part = dot_nt(grad_qkv[m * local : (m + 1) * local], qkv_full)
            total = total + (part if m == 0 else swap(part.astype(BF16), m).astype(F32))
        grad_tokens.append(total)
    grad_qkv_rows = rows_of(grad_qkv_all)
    qkv_weight_grad = dot_tn(rows_of(inputs_all), grad_qkv_rows)
    qkv_bias_grad = jnp.sum(grad_qkv_rows, axis=0, dtype=F32).reshape(pairs, 3, LANES)

    def spread(part):
        return lax.dynamic_update_slice_in_dim(
            jnp.zeros((width,), F32), part.reshape(columns), place * columns, 0
        )

    def summed(name):
        return sum(sums[name])

    inner_bias_grad = lax.dynamic_update_slice_in_dim(
        jnp.zeros((fsdp_size, 2, hidden_part), F32),
        summed("bi").reshape(fsdp_size, 1, hidden_part),
        half,
        1,
    )
    small_grad = jnp.concatenate(
        [
            vector.reshape(fsdp_size, -1)
            for vector in (
                spread(qkv_bias_grad[:, 0]),
                spread(qkv_bias_grad[:, 2]),
                summed("bout"),
                summed("g1"),
                summed("b1"),
                summed("bo"),
                summed("g2"),
                summed("b2"),
                inner_bias_grad,
            )
        ],
        axis=1,
    )
    small_grad = jnp.pad(small_grad, ((0, 0), (0, small_rows * 3 * columns - small_len)))
    last = jnp.concatenate(
        [
            qkv_weight_grad.astype(BF16).reshape(fsdp_size, shard, 3 * columns),
            small_grad.astype(BF16).reshape(fsdp_size, small_rows, 3 * columns),
        ],
        axis=1,
    )
    last = scatter(last.reshape(fsdp_size * (shard + small_rows), 3 * columns))
    qkv_out = jnp.zeros((3, shard, width), F32)
    small_out = jnp.zeros((small_rows, 3 * columns), F32)
    for m in masks:
        piece = (last if m == 0 else swap(last, m)).astype(F32)
        small_out = small_out + piece[shard:]
        block = piece[:shard].reshape(shard, pairs, 3, LANES).transpose(2, 0, 1, 3)
        qkv_out = lax.dynamic_update_slice_in_dim(
            qkv_out, block.reshape(3, shard, columns), (place ^ m) * columns, 2
        )
    small_out = small_out.reshape(-1)
    vectors_out = [small_out[i * shard : (i + 1) * shard] for i in range(8)]
    inner_bias_out = small_out[8 * shard : 8 * shard + hidden_shard]

    def doubled(value, lowest):
        mask = lowest
        while mask < ctx_size:
            value = value.astype(F32) + swap(value.astype(BF16), mask).astype(F32)
            mask *= 2
        return value

    output_grad = doubled(output_shard, 1)

    def both_halves(value):
        mine = doubled(value, 2).astype(BF16)
        theirs = swap(mine, 1)
        first_half = jnp.where(half == 0, mine, theirs).astype(F32)
        second_half = jnp.where(half == 0, theirs, mine).astype(F32)
        return (first_half, second_half)

    outer_grad = jnp.concatenate(both_halves(outer_shard), axis=0)
    inner_parts = [v.reshape(shard, fsdp_size, hidden_part) for v in both_halves(inner_shard)]
    inner_grad = jnp.stack(inner_parts, axis=2).reshape(shard, hidden)
    return (
        jnp.stack([saved[s][7] for s in range(seqs)]),
        jnp.stack(grad_tokens),
        qkv_out[0],
        vectors_out[0],
        qkv_out[1],
        qkv_out[2],
        vectors_out[1],
        output_grad,
        vectors_out[2],
        vectors_out[3],
        vectors_out[4],
        inner_grad,
        inner_bias_out,
        outer_grad,
        vectors_out[5],
        vectors_out[6],
        vectors_out[7],
    )


def solution(mesh):
    row = P("fsdp", None)
    vec = P("fsdp")
    seq = P("fsdp", "ctx", None)
    placed = (
        seq, vec, row, vec, row, row, vec, row, vec, vec, vec, row, vec, row, vec, vec, vec, seq,
    )
    return jax.shard_map(
        functools.partial(body, mesh.shape["ctx"], mesh.shape["fsdp"]),
        mesh=mesh,
        in_specs=placed,
        out_specs=(
            seq, seq, row, vec, row, row, vec, row, vec, vec, vec, row, vec, row, vec, vec, vec,
        ),
        check_vma=False,
    )
```

```python
import functools

import jax
import jax.numpy as jnp
from jax import lax
from jax.experimental import pallas as pl
from jax.experimental.pallas import tpu as pltpu
from jax.sharding import PartitionSpec as P

HEAD_DIM = 64
LANES = 128
EPSILON = 1e-12
ROOT_HALF = 0.7071067811865476
INV_ROOT_TWO_PI = 0.3989422804014327
NEGATIVE = -1e30
BF16 = jnp.bfloat16
F32 = jnp.float32


def normalize(hidden):
    center = hidden - jnp.mean(hidden, axis=-1, keepdims=True)
    variance = jnp.mean(center * center, axis=-1, keepdims=True)
    inverse = lax.rsqrt(variance + EPSILON)
    return (center * inverse, inverse)


def norm_back(grad_norm, normed, inverse):
    mean_grad = jnp.mean(grad_norm, axis=-1, keepdims=True)
    mean_cross = jnp.mean(grad_norm * normed, axis=-1, keepdims=True)
    return inverse * (grad_norm - mean_grad - normed * mean_cross)


def dot_nn(left, right):
    return lax.dot_general(left, right, (((1,), (0,)), ((), ())), preferred_element_type=F32)


def dot_nt(left, right):
    return lax.dot_general(left, right, (((1,), (1,)), ((), ())), preferred_element_type=F32)


def dot_tn(left, right):
    return lax.dot_general(left, right, (((0,), (0,)), ((), ())), preferred_element_type=F32)


def key_bias(scalars, shape, axis, local_len):
    index = lax.broadcasted_iota(jnp.int32, shape, axis)
    owner = jnp.bitwise_xor(scalars[0], index // local_len)
    position = owner * local_len + index % local_len
    return jnp.where(position < scalars[1], 0.0, NEGATIVE).astype(F32)


def head_lanes(values, head):
    lane = lax.broadcasted_iota(jnp.int32, values.shape, 1)
    return jnp.where(lane // HEAD_DIM == head, values, jnp.zeros_like(values))


def attend_kernel(scalars, qkv_ref, out_ref, *, local_len, block):
    total = qkv_ref.shape[0]
    bias = key_bias(scalars, (1, total), 1, local_len)
    keys = qkv_ref[:, LANES : 2 * LANES]
    values = qkv_ref[:, 2 * LANES :]
    masked_values = [head_lanes(values, h) for h in range(2)]

    def step(i, carry):
        rows = pl.ds(pl.multiple_of(i * block, block), block)
        query = qkv_ref[rows, :LANES] * jnp.asarray(HEAD_DIM ** (-0.5), BF16)
        out = None
        for h in range(2):
            scores = dot_nt(head_lanes(query, h), keys) + bias
            top = jnp.max(scores, axis=-1, keepdims=True)
            raw = jnp.exp(scores - top)
            scale = 1.0 / jnp.sum(raw, axis=-1, keepdims=True)
            part = dot_nn((raw * scale).astype(BF16), masked_values[h])
            out = part if out is None else out + part
        out_ref[rows, :] = out.astype(BF16)
        return carry

    lax.fori_loop(0, total // block, step, 0)


def attend_back_kernel(scalars, qkv_ref, grad_ref, out_ref, key_acc, value_acc, *, local_len, block):
    total = qkv_ref.shape[0]
    score_scale = HEAD_DIM ** (-0.5)
    bias = key_bias(scalars, (total, 1), 0, local_len)
    keys = qkv_ref[:, LANES : 2 * LANES]
    values = qkv_ref[:, 2 * LANES :]
    masked_keys = [head_lanes(keys, h) for h in range(2)]
    key_acc[...] = jnp.zeros_like(key_acc)
    value_acc[...] = jnp.zeros_like(value_acc)

    def step(i, carry):
        rows = pl.ds(pl.multiple_of(i * block, block), block)
        query = qkv_ref[rows, :LANES] * jnp.asarray(score_scale, BF16)
        grad = grad_ref[rows, :]
        grad_query = None
        grad_key = None
        grad_value = None
        for h in range(2):
            query_h = head_lanes(query, h)
            grad_h = head_lanes(grad, h)
            scores = dot_nt(keys, query_h) + bias
            top = jnp.max(scores, axis=0, keepdims=True)
            raw = jnp.exp(scores - top)
            weights = raw * (1.0 / jnp.sum(raw, axis=0, keepdims=True))
            grad_probs = dot_nt(values, grad_h)
            inner = jnp.sum(weights * grad_probs, axis=0, keepdims=True)
            grad_scores = (weights * (grad_probs - inner)).astype(BF16)
            part_v = dot_nn(weights.astype(BF16), grad_h)
            part_k = dot_nn(grad_scores, query_h)
            part_q = dot_tn(grad_scores, masked_keys[h])
            grad_value = part_v if h == 0 else grad_value + part_v
            grad_key = part_k if h == 0 else grad_key + part_k
            grad_query = part_q if h == 0 else grad_query + part_q
        out_ref[rows, :LANES] = (grad_query * score_scale).astype(BF16)
        key_acc[...] += grad_key
        value_acc[...] += grad_value
        return carry

    lax.fori_loop(0, total // block, step, 0)
    out_ref[:, LANES : 2 * LANES] = key_acc[...].astype(BF16)
    out_ref[:, 2 * LANES :] = value_acc[...].astype(BF16)


def attend(scalars, qkv, local_len):
    total, width = qkv.shape
    pairs = width // (3 * LANES)
    return pl.pallas_call(
        functools.partial(attend_kernel, local_len=local_len, block=256),
        grid_spec=pltpu.PrefetchScalarGridSpec(
            num_scalar_prefetch=1,
            grid=(pairs,),
            in_specs=[pl.BlockSpec((total, 3 * LANES), lambda j, s: (0, j))],
            out_specs=pl.BlockSpec((total, LANES), lambda j, s: (0, j)),
        ),
        out_shape=jax.ShapeDtypeStruct((total, pairs * LANES), BF16),
        cost_estimate=pl.CostEstimate(flops=13_000_000_000, transcendentals=0, bytes_accessed=4_000_000),
        name="attend",
    )(scalars, qkv)


def attend_back(scalars, qkv, grad, local_len):
    total, width = qkv.shape
    pairs = width // (3 * LANES)
    return pl.pallas_call(
        functools.partial(attend_back_kernel, local_len=local_len, block=256),
        grid_spec=pltpu.PrefetchScalarGridSpec(
            num_scalar_prefetch=1,
            grid=(pairs,),
            in_specs=[
                pl.BlockSpec((total, 3 * LANES), lambda j, s: (0, j)),
                pl.BlockSpec((total, LANES), lambda j, s: (0, j)),
            ],
            out_specs=pl.BlockSpec((total, 3 * LANES), lambda j, s: (0, j)),
            scratch_shapes=[pltpu.VMEM((total, LANES), F32), pltpu.VMEM((total, LANES), F32)],
        ),
        out_shape=jax.ShapeDtypeStruct((total, width), BF16),
        cost_estimate=pl.CostEstimate(flops=23_000_000_000, transcendentals=0, bytes_accessed=4_000_000),
        name="attend_back",
    )(scalars, qkv, grad)


def body(
    ctx_size,
    fsdp_size,
    tokens,
    lengths,
    w_query,
    b_query,
    w_key,
    w_value,
    b_value,
    w_output,
    b_output,
    norm1_gain,
    norm1_bias,
    w_inner,
    b_inner,
    w_outer,
    b_outer,
    norm2_gain,
    norm2_bias,
    cotangent,
):
    place = lax.axis_index("ctx")
    half = place % 2
    seqs, local, width = tokens.shape
    shard = width // fsdp_size
    columns = width // ctx_size
    pairs = columns // LANES
    hidden = w_inner.shape[1]
    hidden_shard = hidden // fsdp_size
    hidden_part = hidden_shard // 2
    masks = range(ctx_size)

    def swap(value, mask):
        return lax.ppermute(value, "ctx", [(i, i ^ mask) for i in range(ctx_size)])

    def head_columns(weight):
        mine = lax.dynamic_slice_in_dim(weight, place * columns, columns, 1)
        return mine.reshape(shard, pairs, LANES)

    qkv_shard = jnp.stack(
        [head_columns(w_query), head_columns(w_key), head_columns(w_value)], axis=2
    ).reshape(shard, 3 * columns)
    output_shard = lax.dynamic_slice_in_dim(w_output, place * columns, columns, 1)
    pack = 4 * columns
    small = jnp.concatenate(
        [
            vector.reshape(-1, shard)
            for vector in (
                b_query, b_value, b_output, norm1_gain, norm1_bias, b_outer, norm2_gain, norm2_bias, b_inner,
            )
        ],
        axis=0,
    ).reshape(-1)
    small_len = small.shape[0]
    small_rows = -(-small_len // pack)
    small_rows = -(-small_rows // 16) * 16
    small = jnp.pad(small, (0, small_rows * pack - small_len)).reshape(small_rows, pack)
    packed = jnp.concatenate([jnp.concatenate([qkv_shard, output_shard], axis=1), small], axis=0)
    first = lax.all_gather(packed, "fsdp", axis=0, tiled=True)
    first = first.reshape(fsdp_size, shard + small_rows, pack)
    qkv_full = first[:, :shard, : 3 * columns].reshape(width, 3 * columns)
    output_part = first[:, :shard, 3 * columns :].reshape(width, columns)
    small_full = first[:, shard:].reshape(fsdp_size, -1).astype(F32)
    vectors = [small_full[:, i * shard : (i + 1) * shard].reshape(width) for i in range(8)]
    query_bias, value_bias, output_bias, gain_one, bias_one, outer_bias, gain_two, bias_two = vectors
    inner_bias = lax.dynamic_index_in_dim(
        small_full[:, 8 * shard : 8 * shard + hidden_shard].reshape(fsdp_size, 2, hidden_part),
        half,
        1,
        keepdims=False,
    ).reshape(fsdp_size * hidden_part)

    def own_bias(vector):
        return lax.dynamic_slice_in_dim(vector, place * columns, columns, 0).reshape(pairs, LANES)

    q_bias, v_bias = (own_bias(query_bias), own_bias(value_bias))
    qkv_bias = jnp.stack([q_bias, jnp.zeros_like(q_bias), v_bias], axis=1).reshape(3 * columns)

    output_full = jnp.zeros((width, width), BF16)
    for m in masks:
        piece = output_part if m == 0 else swap(output_part, m)
        output_full = lax.dynamic_update_slice_in_dim(output_full, piece, (place ^ m) * columns, 1)

    def half_columns(h):
        starts = [(2 * f + h) * hidden_part for f in range(fsdp_size)]
        return jnp.concatenate([w_inner[:, i : i + hidden_part] for i in starts], axis=1)

    inner_half = jnp.where(half == 0, half_columns(0), half_columns(1))
    inner_full = lax.all_gather(inner_half, "fsdp", axis=0, tiled=True)
    outer_half = lax.dynamic_slice_in_dim(w_outer, half * hidden_part, hidden_part, 0)
    outer_full = lax.all_gather(outer_half, "fsdp", axis=0, tiled=True)

    inputs_all, qkv_all, scalars, attn_all = ([], [], [], [])
    for s in range(seqs):
        pieces = [tokens[s] if m == 0 else swap(tokens[s], m) for m in masks]
        inputs_all.append(jnp.concatenate(pieces, axis=0))
        qkv = (dot_nn(inputs_all[s], qkv_full) + qkv_bias).astype(BF16)
        qkv_all.append(qkv)
        scalars.append(jnp.stack([place.astype(jnp.int32), lengths[s]]))
        heads_out = attend(scalars[s], qkv, local)
        attn = jnp.zeros((local, width), BF16)
        for m in masks:
            piece = heads_out[m * local : (m + 1) * local]
            piece = piece if m == 0 else swap(piece, m)
            attn = lax.dynamic_update_slice_in_dim(attn, piece, (place ^ m) * columns, 1)
        attn_all.append(attn)

    saved = []
    for s in range(seqs):
        branch = dot_nn(attn_all[s], output_full) + output_bias
        normed_one, inverse_one = normalize(tokens[s].astype(F32) + branch)
        layer_mid = normed_one * gain_one + bias_one
        mid_low = layer_mid.astype(BF16)
        mids = [mid_low, swap(mid_low, 1)]
        acts, slopes = ([], [])
        for rows in mids:
            pre_act = dot_nn(rows, inner_full) + inner_bias
            erf_part = lax.erf(pre_act * ROOT_HALF)
            acts.append((0.5 * pre_act * (1.0 + erf_part)).astype(BF16))
            slopes.append(
                (
                    0.5 * (1.0 + erf_part)
                    + pre_act * jnp.exp(-0.5 * pre_act * pre_act) * INV_ROOT_TWO_PI
                ).astype(BF16)
            )
        other = swap(dot_nn(acts[1], outer_full).astype(BF16), 1)
        feed_out = dot_nn(acts[0], outer_full) + other.astype(F32) + outer_bias
        normed_two, inverse_two = normalize(layer_mid + feed_out)
        result = (normed_two * gain_two + bias_two).astype(BF16)
        saved.append((normed_one, inverse_one, mids, acts, slopes, normed_two, inverse_two, result))

    sums = {name: [] for name in ("g2", "b2", "bo", "bi", "g1", "b1", "bout")}
    feeds, pres, branches, resid_ones, resid_twos, others = ([], [], [], [], [], [])
    for s in range(seqs):
        normed_two, inverse_two = saved[s][5:7]
        grad_out = cotangent[s].astype(F32)
        sums["g2"].append(jnp.sum(grad_out * normed_two, axis=0))
        sums["b2"].append(jnp.sum(grad_out, axis=0))
        resid_twos.append(norm_back(grad_out * gain_two, normed_two, inverse_two))
        grad_feed = resid_twos[s].astype(BF16)
        sums["bo"].append(jnp.sum(grad_feed, axis=0, dtype=F32))
        grads = [grad_feed, swap(grad_feed, 1)]
        feeds.append(grads)
    for s in range(seqs):
        slopes = saved[s][4]
        pre = [
            (dot_nt(feeds[s][i], outer_full) * slopes[i].astype(F32)).astype(BF16) for i in range(2)
        ]
        pres.append(pre)
        for value in pre:
            sums["bi"].append(jnp.sum(value, axis=0, dtype=F32))
        others.append(swap(dot_nt(pre[1], inner_full).astype(BF16), 1))

    def rows_of(parts):
        return jnp.concatenate(parts, axis=0)

    def scatter(grad):
        return lax.psum_scatter(grad.astype(BF16), "fsdp", scatter_dimension=0, tiled=True)

    act_rows = rows_of([a for s in range(seqs) for a in saved[s][3]])
    mid_rows = rows_of([a for s in range(seqs) for a in saved[s][2]])
    outer_local = dot_tn(act_rows, rows_of([g for pair in feeds for g in pair])).astype(BF16)
    inner_local = dot_tn(mid_rows, rows_of([g for pair in pres for g in pair])).astype(BF16)
    others[0], outer_local = lax.optimization_barrier((others[0], outer_local))
    others[-1], inner_local = lax.optimization_barrier((others[-1], inner_local))
    outer_shard = scatter(outer_local)
    inner_shard = scatter(inner_local)
    for s in range(seqs):
        normed_one, inverse_one = saved[s][:2]
        grad_mid = resid_twos[s] + dot_nt(pres[s][0], inner_full) + others[s].astype(F32)
        sums["g1"].append(jnp.sum(grad_mid * normed_one, axis=0))
        sums["b1"].append(jnp.sum(grad_mid, axis=0))
        grad_resid_one = norm_back(grad_mid * gain_one, normed_one, inverse_one)
        grad_branch = grad_resid_one.astype(BF16)
        sums["bout"].append(jnp.sum(grad_branch, axis=0, dtype=F32))
        resid_ones.append(grad_resid_one)
        branches.append(grad_branch)
    output_local = dot_tn(rows_of(attn_all), rows_of(branches)).astype(BF16)

    grad_qkv_all, grad_tokens, token_parts = ([], [], [])
    for s in range(seqs):
        grad_attn = dot_nt(branches[s], output_full).astype(BF16)
        pieces = []
        for m in masks:
            piece = lax.dynamic_slice_in_dim(grad_attn, (place ^ m) * columns, columns, 1)
            pieces.append(piece if m == 0 else swap(piece, m))
        rows = rows_of(pieces)
        if s == 0:
            rows, output_local = lax.optimization_barrier((rows, output_local))
        else:
            rows, outer_shard = lax.optimization_barrier((rows, outer_shard))
        grad_qkv = attend_back(scalars[s], qkv_all[s], rows, local)
        grad_qkv_all.append(grad_qkv)
        if s == 0:
            output_parts = [
                lax.dynamic_slice_in_dim(output_local, (place ^ m) * columns, columns, 1) for m in masks
            ]
            output_parts = [p if m == 0 else swap(p, m) for m, p in zip(masks, output_parts)]
        parts = [dot_nt(grad_qkv[m * local : (m + 1) * local], qkv_full) for m in masks]
        token_parts.append([p if m == 0 else swap(p.astype(BF16), m) for m, p in zip(masks, parts)])
        if s > 0:
            tied = lax.optimization_barrier((grad_qkv, token_parts[s - 1], output_parts))
            grad_qkv_all[s], token_parts[s - 1], output_parts = tied
    for s in range(seqs):
        total = resid_ones[s]
        for part in token_parts[s]:
            total = total + part.astype(F32)
        grad_tokens.append(total)
    grad_qkv_rows = rows_of(grad_qkv_all)
    qkv_weight_grad = dot_tn(rows_of(inputs_all), grad_qkv_rows)
    qkv_bias_grad = jnp.sum(grad_qkv_rows, axis=0, dtype=F32).reshape(pairs, 3, LANES)

    def spread(part):
        return lax.dynamic_update_slice_in_dim(
            jnp.zeros((width,), F32), part.reshape(columns), place * columns, 0
        )

    def summed(name):
        return sum(sums[name])

    inner_bias_grad = lax.dynamic_update_slice_in_dim(
        jnp.zeros((fsdp_size, 2, hidden_part), F32),
        summed("bi").reshape(fsdp_size, 1, hidden_part),
        half,
        1,
    )
    small_grad = jnp.concatenate(
        [
            vector.reshape(fsdp_size, -1)
            for vector in (
                spread(qkv_bias_grad[:, 0]),
                spread(qkv_bias_grad[:, 2]),
                summed("bout"),
                summed("g1"),
                summed("b1"),
                summed("bo"),
                summed("g2"),
                summed("b2"),
                inner_bias_grad,
            )
        ],
        axis=1,
    )
    small_grad = jnp.pad(small_grad, ((0, 0), (0, small_rows * pack - small_len)))
    output_sum = None
    for piece in output_parts:
        output_sum = piece.astype(F32) if output_sum is None else output_sum + piece.astype(F32)
    weight_grads = jnp.concatenate([qkv_weight_grad.astype(BF16), output_sum.astype(BF16)], axis=1)
    last = jnp.concatenate(
        [
            weight_grads.reshape(fsdp_size, shard, pack),
            small_grad.astype(BF16).reshape(fsdp_size, small_rows, pack),
        ],
        axis=1,
    )
    last, inner_shard = lax.optimization_barrier((last, inner_shard))
    last = scatter(last.reshape(fsdp_size * (shard + small_rows), pack))
    outs = [jnp.zeros((shard, width), F32) for _ in range(4)]
    small_out = jnp.zeros((small_rows, pack), F32)
    for m in masks:
        piece = (last if m == 0 else swap(last, m)).astype(F32)
        small_out = small_out + piece[shard:]
        at = (place ^ m) * columns
        for t in range(4):
            if t == 3:
                block = piece[:shard, 3 * columns :]
            else:
                starts = [(3 * j + t) * LANES for j in range(pairs)]
                block = jnp.concatenate([piece[:shard, i : i + LANES] for i in starts], axis=1)
            outs[t] = lax.dynamic_update_slice_in_dim(outs[t], block, at, 1)
    small_out = small_out.reshape(-1)
    vectors_out = [small_out[i * shard : (i + 1) * shard] for i in range(8)]
    inner_bias_out = small_out[8 * shard : 8 * shard + hidden_shard]

    def doubled(value, lowest):
        mask = lowest
        while mask < ctx_size:
            value = value.astype(F32) + swap(value.astype(BF16), mask).astype(F32)
            mask *= 2
        return value

    def both_halves(value):
        mine = doubled(value, 2).astype(BF16)
        theirs = swap(mine, 1)
        first_half = jnp.where(half == 0, mine, theirs).astype(F32)
        second_half = jnp.where(half == 0, theirs, mine).astype(F32)
        return (first_half, second_half)

    outer_grad = jnp.concatenate(both_halves(outer_shard), axis=0)
    inner_parts = both_halves(inner_shard)
    inner_grad = jnp.concatenate(
        [
            part[:, f * hidden_part : (f + 1) * hidden_part]
            for f in range(fsdp_size)
            for part in inner_parts
        ],
        axis=1,
    )
    return (
        jnp.stack([saved[s][7] for s in range(seqs)]),
        jnp.stack(grad_tokens),
        outs[0],
        vectors_out[0],
        outs[1],
        outs[2],
        vectors_out[1],
        outs[3],
        vectors_out[2],
        vectors_out[3],
        vectors_out[4],
        inner_grad,
        inner_bias_out,
        outer_grad,
        vectors_out[5],
        vectors_out[6],
        vectors_out[7],
    )


def solution(mesh):
    row = P("fsdp", None)
    vec = P("fsdp")
    seq = P("fsdp", "ctx", None)
    placed = (
        seq, vec, row, vec, row, row, vec, row, vec, vec, vec, row, vec, row, vec, vec, vec, seq,
    )
    return jax.shard_map(
        functools.partial(body, mesh.shape["ctx"], mesh.shape["fsdp"]),
        mesh=mesh,
        in_specs=placed,
        out_specs=(
            seq, seq, row, vec, row, row, vec, row, vec, vec, vec, row, vec, row, vec, vec, vec,
        ),
        check_vma=False,
    )
```

```python
import functools

import jax
import jax.numpy as jnp
from jax import lax
from jax.experimental import pallas as pl
from jax.experimental.pallas import tpu as pltpu
from jax.sharding import PartitionSpec as P

HEAD_DIM = 64
LANES = 128
EPSILON = 1e-12
ROOT_HALF = 0.7071067811865476
INV_ROOT_TWO_PI = 0.3989422804014327
NEGATIVE = -1e30
BF16 = jnp.bfloat16
F32 = jnp.float32


def normalize(hidden):
    center = hidden - jnp.mean(hidden, axis=-1, keepdims=True)
    variance = jnp.mean(center * center, axis=-1, keepdims=True)
    inverse = lax.rsqrt(variance + EPSILON)
    return (center * inverse, inverse)


def norm_back(grad_norm, normed, inverse):
    mean_grad = jnp.mean(grad_norm, axis=-1, keepdims=True)
    mean_cross = jnp.mean(grad_norm * normed, axis=-1, keepdims=True)
    return inverse * (grad_norm - mean_grad - normed * mean_cross)


def dot_nn(left, right):
    return lax.dot_general(left, right, (((1,), (0,)), ((), ())), preferred_element_type=F32)


def dot_nt(left, right):
    return lax.dot_general(left, right, (((1,), (1,)), ((), ())), preferred_element_type=F32)


def dot_tn(left, right):
    return lax.dot_general(left, right, (((0,), (0,)), ((), ())), preferred_element_type=F32)


def key_bias(scalars, shape, axis, local_len):
    index = lax.broadcasted_iota(jnp.int32, shape, axis)
    owner = jnp.bitwise_xor(scalars[0], index // local_len)
    position = owner * local_len + index % local_len
    return jnp.where(position < scalars[1], 0.0, NEGATIVE).astype(F32)


def head_lanes(values, head):
    lane = lax.broadcasted_iota(jnp.int32, values.shape, 1)
    return jnp.where(lane // HEAD_DIM == head, values, jnp.zeros_like(values))


def attend_kernel(scalars, qkv_ref, out_ref, *, local_len, block):
    total = qkv_ref.shape[0]
    bias = key_bias(scalars, (1, total), 1, local_len)
    keys = qkv_ref[:, LANES : 2 * LANES]
    values = qkv_ref[:, 2 * LANES :]
    masked_values = [head_lanes(values, h) for h in range(2)]

    def step(i, carry):
        rows = pl.ds(pl.multiple_of(i * block, block), block)
        query = qkv_ref[rows, :LANES] * jnp.asarray(HEAD_DIM ** (-0.5), BF16)
        out = None
        for h in range(2):
            scores = dot_nt(head_lanes(query, h), keys) + bias
            top = jnp.max(scores, axis=-1, keepdims=True)
            raw = jnp.exp(scores - top)
            scale = 1.0 / jnp.sum(raw, axis=-1, keepdims=True)
            part = dot_nn((raw * scale).astype(BF16), masked_values[h])
            out = part if out is None else out + part
        out_ref[rows, :] = out.astype(BF16)
        return carry

    lax.fori_loop(0, total // block, step, 0)


def attend_back_kernel(scalars, qkv_ref, grad_ref, out_ref, key_acc, value_acc, *, local_len, block):
    total = qkv_ref.shape[0]
    score_scale = HEAD_DIM ** (-0.5)
    bias = key_bias(scalars, (total, 1), 0, local_len)
    keys = qkv_ref[:, LANES : 2 * LANES]
    values = qkv_ref[:, 2 * LANES :]
    masked_keys = [head_lanes(keys, h) for h in range(2)]
    key_acc[...] = jnp.zeros_like(key_acc)
    value_acc[...] = jnp.zeros_like(value_acc)

    def step(i, carry):
        rows = pl.ds(pl.multiple_of(i * block, block), block)
        query = qkv_ref[rows, :LANES] * jnp.asarray(score_scale, BF16)
        grad = grad_ref[rows, :]
        grad_query = None
        grad_key = None
        grad_value = None
        for h in range(2):
            query_h = head_lanes(query, h)
            grad_h = head_lanes(grad, h)
            scores = dot_nt(keys, query_h) + bias
            top = jnp.max(scores, axis=0, keepdims=True)
            raw = jnp.exp(scores - top)
            weights = raw * (1.0 / jnp.sum(raw, axis=0, keepdims=True))
            grad_probs = dot_nt(values, grad_h)
            inner = jnp.sum(weights * grad_probs, axis=0, keepdims=True)
            grad_scores = (weights * (grad_probs - inner)).astype(BF16)
            part_v = dot_nn(weights.astype(BF16), grad_h)
            part_k = dot_nn(grad_scores, query_h)
            part_q = dot_tn(grad_scores, masked_keys[h])
            grad_value = part_v if h == 0 else grad_value + part_v
            grad_key = part_k if h == 0 else grad_key + part_k
            grad_query = part_q if h == 0 else grad_query + part_q
        out_ref[rows, :LANES] = (grad_query * score_scale).astype(BF16)
        key_acc[...] += grad_key
        value_acc[...] += grad_value
        return carry

    lax.fori_loop(0, total // block, step, 0)
    out_ref[:, LANES : 2 * LANES] = key_acc[...].astype(BF16)
    out_ref[:, 2 * LANES :] = value_acc[...].astype(BF16)


def attend(scalars, qkv, local_len):
    total, width = qkv.shape
    pairs = width // (3 * LANES)
    return pl.pallas_call(
        functools.partial(attend_kernel, local_len=local_len, block=256),
        grid_spec=pltpu.PrefetchScalarGridSpec(
            num_scalar_prefetch=1,
            grid=(pairs,),
            in_specs=[pl.BlockSpec((total, 3 * LANES), lambda j, s: (0, j))],
            out_specs=pl.BlockSpec((total, LANES), lambda j, s: (0, j)),
        ),
        out_shape=jax.ShapeDtypeStruct((total, pairs * LANES), BF16),
        cost_estimate=pl.CostEstimate(flops=13_000_000_000, transcendentals=0, bytes_accessed=4_000_000),
        name="attend",
    )(scalars, qkv)


def attend_back(scalars, qkv, grad, local_len):
    total, width = qkv.shape
    pairs = width // (3 * LANES)
    return pl.pallas_call(
        functools.partial(attend_back_kernel, local_len=local_len, block=256),
        grid_spec=pltpu.PrefetchScalarGridSpec(
            num_scalar_prefetch=1,
            grid=(pairs,),
            in_specs=[
                pl.BlockSpec((total, 3 * LANES), lambda j, s: (0, j)),
                pl.BlockSpec((total, LANES), lambda j, s: (0, j)),
            ],
            out_specs=pl.BlockSpec((total, 3 * LANES), lambda j, s: (0, j)),
            scratch_shapes=[pltpu.VMEM((total, LANES), F32), pltpu.VMEM((total, LANES), F32)],
        ),
        out_shape=jax.ShapeDtypeStruct((total, width), BF16),
        cost_estimate=pl.CostEstimate(flops=23_000_000_000, transcendentals=0, bytes_accessed=4_000_000),
        name="attend_back",
    )(scalars, qkv, grad)


def body(
    ctx_size,
    fsdp_size,
    tokens,
    lengths,
    w_query,
    b_query,
    w_key,
    w_value,
    b_value,
    w_output,
    b_output,
    norm1_gain,
    norm1_bias,
    w_inner,
    b_inner,
    w_outer,
    b_outer,
    norm2_gain,
    norm2_bias,
    cotangent,
):
    place = lax.axis_index("ctx")
    half = place % 2
    seqs, local, width = tokens.shape
    shard = width // fsdp_size
    columns = width // ctx_size
    pairs = columns // LANES
    hidden = w_inner.shape[1]
    hidden_shard = hidden // fsdp_size
    hidden_part = hidden_shard // 2
    masks = range(ctx_size)

    def swap(value, mask):
        return lax.ppermute(value, "ctx", [(i, i ^ mask) for i in range(ctx_size)])

    def head_columns(weight):
        mine = lax.dynamic_slice_in_dim(weight, place * columns, columns, 1)
        return mine.reshape(shard, pairs, LANES)

    qkv_shard = jnp.stack(
        [head_columns(w_query), head_columns(w_key), head_columns(w_value)], axis=2
    ).reshape(shard, 3 * columns)
    output_shard = lax.dynamic_slice_in_dim(w_output, place * columns, columns, 1)
    pack = 4 * columns
    small = jnp.concatenate(
        [
            vector.reshape(-1, shard)
            for vector in (
                b_query, b_value, b_output, norm1_gain, norm1_bias, b_outer, norm2_gain, norm2_bias, b_inner,
            )
        ],
        axis=0,
    ).reshape(-1)
    small_len = small.shape[0]
    small_rows = -(-small_len // pack)
    small_rows = -(-small_rows // 16) * 16
    small = jnp.pad(small, (0, small_rows * pack - small_len)).reshape(small_rows, pack)
    packed = jnp.concatenate([jnp.concatenate([qkv_shard, output_shard], axis=1), small], axis=0)
    first = lax.all_gather(packed, "fsdp", axis=0, tiled=True)
    first = first.reshape(fsdp_size, shard + small_rows, pack)
    qkv_full = first[:, :shard, : 3 * columns].reshape(width, 3 * columns)
    output_part = first[:, :shard, 3 * columns :].reshape(width, columns)
    small_full = first[:, shard:].reshape(fsdp_size, -1).astype(F32)
    vectors = [small_full[:, i * shard : (i + 1) * shard].reshape(width) for i in range(8)]
    query_bias, value_bias, output_bias, gain_one, bias_one, outer_bias, gain_two, bias_two = vectors
    inner_bias = lax.dynamic_index_in_dim(
        small_full[:, 8 * shard : 8 * shard + hidden_shard].reshape(fsdp_size, 2, hidden_part),
        half,
        1,
        keepdims=False,
    ).reshape(fsdp_size * hidden_part)

    def own_bias(vector):
        return lax.dynamic_slice_in_dim(vector, place * columns, columns, 0).reshape(pairs, LANES)

    q_bias, v_bias = (own_bias(query_bias), own_bias(value_bias))
    qkv_bias = jnp.stack([q_bias, jnp.zeros_like(q_bias), v_bias], axis=1).reshape(3 * columns)

    output_full = jnp.zeros((width, width), BF16)
    for m in masks:
        piece = output_part if m == 0 else swap(output_part, m)
        output_full = lax.dynamic_update_slice_in_dim(output_full, piece, (place ^ m) * columns, 1)

    inner_half = lax.dynamic_index_in_dim(
        w_inner.reshape(shard, fsdp_size, 2, hidden_part), half, 2, keepdims=False
    ).reshape(shard, fsdp_size * hidden_part)
    inner_full = lax.all_gather(inner_half, "fsdp", axis=0, tiled=True)
    outer_half = lax.dynamic_slice_in_dim(w_outer, half * hidden_part, hidden_part, 0)
    outer_full = lax.all_gather(outer_half, "fsdp", axis=0, tiled=True)

    inputs_all, qkv_all, scalars, attn_all = ([], [], [], [])
    for s in range(seqs):
        pieces = [tokens[s] if m == 0 else swap(tokens[s], m) for m in masks]
        inputs_all.append(jnp.concatenate(pieces, axis=0))
        qkv = (dot_nn(inputs_all[s], qkv_full) + qkv_bias).astype(BF16)
        qkv_all.append(qkv)
        scalars.append(jnp.stack([place.astype(jnp.int32), lengths[s]]))
        heads_out = attend(scalars[s], qkv, local)
        attn = jnp.zeros((local, width), BF16)
        for m in masks:
            piece = heads_out[m * local : (m + 1) * local]
            piece = piece if m == 0 else swap(piece, m)
            attn = lax.dynamic_update_slice_in_dim(attn, piece, (place ^ m) * columns, 1)
        attn_all.append(attn)

    saved = []
    for s in range(seqs):
        branch = dot_nn(attn_all[s], output_full) + output_bias
        normed_one, inverse_one = normalize(tokens[s].astype(F32) + branch)
        layer_mid = normed_one * gain_one + bias_one
        mid_low = layer_mid.astype(BF16)
        mids = [mid_low, swap(mid_low, 1)]
        acts, slopes = ([], [])
        for rows in mids:
            pre_act = dot_nn(rows, inner_full) + inner_bias
            erf_part = lax.erf(pre_act * ROOT_HALF)
            acts.append((0.5 * pre_act * (1.0 + erf_part)).astype(BF16))
            slopes.append(
                (
                    0.5 * (1.0 + erf_part)
                    + pre_act * jnp.exp(-0.5 * pre_act * pre_act) * INV_ROOT_TWO_PI
                ).astype(BF16)
            )
        other = swap(dot_nn(acts[1], outer_full).astype(BF16), 1)
        feed_out = dot_nn(acts[0], outer_full) + other.astype(F32) + outer_bias
        normed_two, inverse_two = normalize(layer_mid + feed_out)
        result = (normed_two * gain_two + bias_two).astype(BF16)
        saved.append((normed_one, inverse_one, mids, acts, slopes, normed_two, inverse_two, result))

    sums = {name: [] for name in ("g2", "b2", "bo", "bi", "g1", "b1", "bout")}
    feeds, pres, branches, resid_ones, resid_twos, others = ([], [], [], [], [], [])
    for s in range(seqs):
        normed_two, inverse_two = saved[s][5:7]
        grad_out = cotangent[s].astype(F32)
        sums["g2"].append(jnp.sum(grad_out * normed_two, axis=0))
        sums["b2"].append(jnp.sum(grad_out, axis=0))
        resid_twos.append(norm_back(grad_out * gain_two, normed_two, inverse_two))
        grad_feed = resid_twos[s].astype(BF16)
        sums["bo"].append(jnp.sum(grad_feed, axis=0, dtype=F32))
        grads = [grad_feed, swap(grad_feed, 1)]
        feeds.append(grads)
    for s in range(seqs):
        slopes = saved[s][4]
        pre = [
            (dot_nt(feeds[s][i], outer_full) * slopes[i].astype(F32)).astype(BF16) for i in range(2)
        ]
        pres.append(pre)
        for value in pre:
            sums["bi"].append(jnp.sum(value, axis=0, dtype=F32))
        others.append(swap(dot_nt(pre[1], inner_full).astype(BF16), 1))

    def rows_of(parts):
        return jnp.concatenate(parts, axis=0)

    def scatter(grad):
        return lax.psum_scatter(grad.astype(BF16), "fsdp", scatter_dimension=0, tiled=True)

    act_rows = rows_of([a for s in range(seqs) for a in saved[s][3]])
    mid_rows = rows_of([a for s in range(seqs) for a in saved[s][2]])
    outer_local = dot_tn(act_rows, rows_of([g for pair in feeds for g in pair])).astype(BF16)
    inner_local = dot_tn(mid_rows, rows_of([g for pair in pres for g in pair])).astype(BF16)
    others[0], outer_local = lax.optimization_barrier((others[0], outer_local))
    others[-1], inner_local = lax.optimization_barrier((others[-1], inner_local))
    outer_shard = scatter(outer_local)
    inner_shard = scatter(inner_local)
    for s in range(seqs):
        normed_one, inverse_one = saved[s][:2]
        grad_mid = resid_twos[s] + dot_nt(pres[s][0], inner_full) + others[s].astype(F32)
        sums["g1"].append(jnp.sum(grad_mid * normed_one, axis=0))
        sums["b1"].append(jnp.sum(grad_mid, axis=0))
        grad_resid_one = norm_back(grad_mid * gain_one, normed_one, inverse_one)
        grad_branch = grad_resid_one.astype(BF16)
        sums["bout"].append(jnp.sum(grad_branch, axis=0, dtype=F32))
        resid_ones.append(grad_resid_one)
        branches.append(grad_branch)
    output_local = dot_tn(rows_of(attn_all), rows_of(branches)).astype(BF16)

    grad_qkv_all, grad_tokens, token_parts = ([], [], [])
    for s in range(seqs):
        grad_attn = dot_nt(branches[s], output_full).astype(BF16)
        pieces = []
        for m in masks:
            piece = lax.dynamic_slice_in_dim(grad_attn, (place ^ m) * columns, columns, 1)
            pieces.append(piece if m == 0 else swap(piece, m))
        rows = rows_of(pieces)
        if s == 0:
            rows, output_local = lax.optimization_barrier((rows, output_local))
        else:
            rows, outer_shard = lax.optimization_barrier((rows, outer_shard))
        grad_qkv = attend_back(scalars[s], qkv_all[s], rows, local)
        grad_qkv_all.append(grad_qkv)
        if s == 0:
            output_parts = [
                lax.dynamic_slice_in_dim(output_local, (place ^ m) * columns, columns, 1) for m in masks
            ]
            output_parts = [p if m == 0 else swap(p, m) for m, p in zip(masks, output_parts)]
        parts = [dot_nt(grad_qkv[m * local : (m + 1) * local], qkv_full) for m in masks]
        token_parts.append([p if m == 0 else swap(p.astype(BF16), m) for m, p in zip(masks, parts)])
        if s > 0:
            tied = lax.optimization_barrier((grad_qkv, token_parts[s - 1]))
            grad_qkv_all[s], token_parts[s - 1] = tied
    for s in range(seqs):
        total = resid_ones[s]
        for part in token_parts[s]:
            total = total + part.astype(F32)
        grad_tokens.append(total)
    grad_qkv_rows = rows_of(grad_qkv_all)
    qkv_weight_grad = dot_tn(rows_of(inputs_all), grad_qkv_rows).astype(BF16)
    qkv_weight_grad, output_parts = lax.optimization_barrier((qkv_weight_grad, output_parts))
    qkv_bias_grad = jnp.sum(grad_qkv_rows, axis=0, dtype=F32).reshape(pairs, 3, LANES)

    def spread(part):
        return lax.dynamic_update_slice_in_dim(
            jnp.zeros((width,), F32), part.reshape(columns), place * columns, 0
        )

    def summed(name):
        return sum(sums[name])

    inner_bias_grad = lax.dynamic_update_slice_in_dim(
        jnp.zeros((fsdp_size, 2, hidden_part), F32),
        summed("bi").reshape(fsdp_size, 1, hidden_part),
        half,
        1,
    )
    small_grad = jnp.concatenate(
        [
            vector.reshape(fsdp_size, -1)
            for vector in (
                spread(qkv_bias_grad[:, 0]),
                spread(qkv_bias_grad[:, 2]),
                summed("bout"),
                summed("g1"),
                summed("b1"),
                summed("bo"),
                summed("g2"),
                summed("b2"),
                inner_bias_grad,
            )
        ],
        axis=1,
    )
    small_grad = jnp.pad(small_grad, ((0, 0), (0, small_rows * pack - small_len)))
    output_sum = None
    for piece in output_parts:
        output_sum = piece.astype(F32) if output_sum is None else output_sum + piece.astype(F32)
    weight_grads = jnp.concatenate([qkv_weight_grad, output_sum.astype(BF16)], axis=1)
    last = jnp.concatenate(
        [
            weight_grads.reshape(fsdp_size, shard, pack),
            small_grad.astype(BF16).reshape(fsdp_size, small_rows, pack),
        ],
        axis=1,
    )
    last, inner_shard = lax.optimization_barrier((last, inner_shard))
    last = scatter(last.reshape(fsdp_size * (shard + small_rows), pack))

    def paired(value):
        mask = 2
        while mask < ctx_size:
            value = value.astype(F32) + swap(value.astype(BF16), mask).astype(F32)
            mask *= 2
        mine = value.astype(BF16)
        return (mine, swap(mine, 1))

    outer_mine, inner_mine = (paired(outer_shard), paired(inner_shard))
    last, mines = lax.optimization_barrier((last, (outer_mine[0], inner_mine[0])))
    outer_mine, inner_mine = ((mines[0], outer_mine[1]), (mines[1], inner_mine[1]))
    outs = [jnp.zeros((shard, width), F32) for _ in range(4)]
    small_out = jnp.zeros((small_rows, pack), F32)
    for m in masks:
        piece = (last if m == 0 else swap(last, m)).astype(F32)
        small_out = small_out + piece[shard:]
        at = (place ^ m) * columns
        for t in range(4):
            if t == 3:
                block = piece[:shard, 3 * columns :]
            else:
                starts = [(3 * j + t) * LANES for j in range(pairs)]
                block = jnp.concatenate([piece[:shard, i : i + LANES] for i in starts], axis=1)
            outs[t] = lax.dynamic_update_slice_in_dim(outs[t], block, at, 1)
    small_out = small_out.reshape(-1)
    vectors_out = [small_out[i * shard : (i + 1) * shard] for i in range(8)]
    inner_bias_out = small_out[8 * shard : 8 * shard + hidden_shard]

    def both_halves(pair):
        mine, theirs = pair
        first_half = jnp.where(half == 0, mine, theirs).astype(F32)
        second_half = jnp.where(half == 0, theirs, mine).astype(F32)
        return (first_half, second_half)

    outer_grad = jnp.concatenate(both_halves(outer_mine), axis=0)
    inner_parts = [v.reshape(shard, fsdp_size, hidden_part) for v in both_halves(inner_mine)]
    inner_grad = jnp.stack(inner_parts, axis=2).reshape(shard, hidden)
    return (
        jnp.stack([saved[s][7] for s in range(seqs)]),
        jnp.stack(grad_tokens),
        outs[0],
        vectors_out[0],
        outs[1],
        outs[2],
        vectors_out[1],
        outs[3],
        vectors_out[2],
        vectors_out[3],
        vectors_out[4],
        inner_grad,
        inner_bias_out,
        outer_grad,
        vectors_out[5],
        vectors_out[6],
        vectors_out[7],
    )


def solution(mesh):
    row = P("fsdp", None)
    vec = P("fsdp")
    seq = P("fsdp", "ctx", None)
    placed = (
        seq, vec, row, vec, row, row, vec, row, vec, vec, vec, row, vec, row, vec, vec, vec, seq,
    )
    return jax.shard_map(
        functools.partial(body, mesh.shape["ctx"], mesh.shape["fsdp"]),
        mesh=mesh,
        in_specs=placed,
        out_specs=(
            seq, seq, row, vec, row, row, vec, row, vec, vec, vec, row, vec, row, vec, vec, vec,
        ),
        check_vma=False,
    )
```
